32 devices in a mesh: groups: 2 (over y), seq: 4 (over z), req: 2 (over x), head: 2 (over core).
Axes of the slice: x: 2, y: 2, z: 4, core: 2. Of those that a mesh axis runs over, the one named last changes fastest.
Arguments:
- cache: bfloat16 [8, 6144, 576], P(('groups', 'req'), 'seq'), parts along dimension 0, may hold values from -4 to 4
- index_key: bfloat16 [8, 6144, 128], P(('groups', 'req'), 'seq'), parts along dimension 0, may hold values from -4 to 4
- index_scale: float32 [8, 6144], P(('groups', 'req'), 'seq'), parts along dimension 0, may hold values from 1.5 to 12
- lengths: int32 [8], P(('groups', 'req')), parts along dimension 0, may hold values from 4608 to 6143, as said below
- owners: int32 [8], P(('groups', 'req')), parts along dimension 0, may hold values from 0 to 3, as said below
- selected: int32 [2, 8, 2048], P(None, ('groups', 'req')), parts along dimension 1, may hold values from 0 to 6143, as said below
- query: bfloat16 [2, 16, 128, 576], P(None, ('groups', 'seq', 'req'), 'head'), parts along dimension 1, may hold values from -41 to 41
- index_query: bfloat16 [2, 16, 64, 128], P(None, ('groups', 'seq', 'req')), parts along dimension 1, may hold values from -0.5 to 0.5
- index_weight: bfloat16 [2, 16, 64], P(None, ('groups', 'seq', 'req')), parts along dimension 1, may hold values from -0.75 to 0.75
Outputs:
- index_scores: float32 [2, 8, 6144], P(None, ('groups', 'req'), 'seq'), parts along dimension 1
- threshold: float32 [2, 8], P(None, ('groups', 'req')), parts along dimension 1
- attended: bfloat16 [2, 16, 128, 512], P(None, ('groups', 'seq', 'req'), 'head'), parts along dimension 1
The draws below stay inside these ranges and needn't reach their ends.
There are 2 independent parts, one for each index of `groups`. The reference program is written for one: setup_inputs(seed, part) draws one part's arguments, and reference() takes and returns one part's arrays. A program takes and returns all parts, laid end to end along the dimension named above; each array names one. Nothing has to cross between parts.
Inputs may be any that keep to these rules, and one draw needn't show every extreme that they name: `lengths`: some request of each group has length 6143. The 2 requests i * 2 to (i + 1) * 2 - 1 have distinct owners. selected[t, r] holds 2048 distinct positions below lengths[r] + t; at most 768 of them lie in one block of positions k * 1536 to (k + 1) * 1536 - 1, and in every list some block holds exactly 768.
All inputs are finite; a program needn't handle non-finite values.
Results may differ from the reference program's by a relative error of at most 0.007.
Values may be sent and summed in bfloat16 or wider, within the bound.
No kernel may reach another device: no remote copies, remote signals or barrier semaphores. Data moves between devices by JAX's collectives and lax.ppermute only.
A program may use at most 64 MiB of HBM per device.

```python
import math
import jax
import jax.numpy as jnp
from jax import lax

H = 128
LAT = 512
ROPE = 64
IH = 64
IDK = 128
TOPK = 2048
CTX = 6144
STEPS = 2
REQ_COL = 2
REQS = 4
SH = 1536
CAP = 768
LEN_MIN = 4608
SLOTS = 8
N_SEQ = 4
N_REQ = 2


def length_draw(key):
    spread = jax.random.randint(jax.random.fold_in(key, 101), (REQS,), LEN_MIN, CTX)
    order = jax.random.permutation(jax.random.fold_in(key, 102), REQS)
    spread = spread.at[order[0]].set(CTX - 1)
    spread = spread.at[order[1]].set(LEN_MIN)
    return spread.astype(jnp.int32)


def owner_draw(key):
    column_keys = jax.random.split(jax.random.fold_in(key, 201), N_REQ)

    def column(subkey):
        return jax.random.permutation(subkey, N_SEQ)[:REQ_COL]
    return jax.vmap(column)(column_keys).reshape(REQS).astype(jnp.int32)


def one_list(list_key, length):
    full = length // SH
    heavy_key, perm_key, order_key = jax.random.split(list_key, 3)
    heavy = jax.random.randint(heavy_key, (), 0, full)
    shard = jnp.arange(N_SEQ, dtype=jnp.int32)
    rest = TOPK - CAP
    base_count = rest // (full - 1)
    extra = rest % (full - 1)
    among = shard - (shard > heavy).astype(jnp.int32)
    counts = jnp.where(shard == heavy, CAP, jnp.where(shard < full, base_count + (among < extra).astype(jnp.int32), 0))
    perm_keys = jax.random.split(perm_key, N_SEQ)
    perms = jax.vmap(lambda subkey: jax.random.permutation(subkey, SH))(perm_keys)
    ranks = jnp.argsort(perms, axis=1)
    chosen = (ranks < counts[:, None]).reshape(CTX)
    picked = jnp.nonzero(chosen, size=TOPK, fill_value=0)[0]
    return picked[jax.random.permutation(order_key, TOPK)].astype(jnp.int32)


def selection_draw(key):
    lengths = length_draw(key)
    list_keys = jax.random.split(jax.random.fold_in(key, 301), STEPS * REQS)
    step_lengths = lengths[None, :] + jnp.arange(STEPS, dtype=jnp.int32)[:, None]
    lists = jax.vmap(one_list)(list_keys, step_lengths.reshape(STEPS * REQS))
    return lists.reshape(STEPS, REQS, TOPK)


def cache_rows(key, flat_index):
    base_key = jax.random.fold_in(key, 401)

    def row_draw(index):
        row_key = jax.random.fold_in(base_key, index)
        values = jnp.clip(jax.random.normal(row_key, (LAT + ROPE,)), -4.0, 4.0)
        return values.astype(jnp.bfloat16).astype(jnp.float32)
    rows = jax.vmap(row_draw)(flat_index.reshape(-1))
    return rows.reshape(flat_index.shape + (LAT + ROPE,))


def draw_cache(key, part):
    rows = cache_rows(key, jnp.arange(REQS * CTX, dtype=jnp.int32))
    return rows.reshape(REQS, CTX, LAT + ROPE).astype(jnp.bfloat16)


def draw_lengths(key, part):
    return length_draw(key)


def draw_owners(key, part):
    return owner_draw(key)


def draw_selected(key, part):
    return selection_draw(key)


def draw_query(key, part):
    shape = (STEPS, SLOTS, H, LAT + ROPE)
    values = jnp.clip(1.2 * jax.random.normal(jax.random.fold_in(key, 501), shape), -4.8, 4.8)
    return values.astype(jnp.bfloat16)


def levels(rng, extent, cuts, smallest, high):
    loudness, own = 1.0, jax.random.fold_in(rng, 6)
    for dim, parts in cuts:
        heights = jnp.exp(jax.random.uniform(jax.random.fold_in(own, dim), (parts,), jnp.float32, smallest / len(cuts), high / len(cuts)))
        loudness = loudness * jnp.repeat(heights, extent[dim] // parts).reshape([-1 if axis == dim else 1 for axis in range(len(extent))])
    return loudness


def centred(rng, dims, deviation, bound, pieces=(), kind=jnp.bfloat16):
    values = deviation * jax.random.normal(rng, dims, jnp.float32)
    if pieces:
        values = values * levels(rng, dims, pieces, -0.22, 0.18)
    return jnp.clip(values, -bound, bound).astype(kind)


def setup_inputs(seed: int = 0, part: int = 0) -> dict:
    keys = jax.random.split(jax.random.key(seed), 10)
    part_keys = jax.random.split(jax.random.fold_in(keys[9], part), 10)
    return {
        "cache": draw_cache(jax.random.fold_in(jax.random.fold_in(keys[9], part), 71), part),
        "index_key": centred(part_keys[1], (REQS, CTX, IDK), 1.0, 4.0, ((0, 2), (1, 4))),
        "index_scale": jnp.clip(jnp.exp(math.log(12.0) - 2.0794415 * jax.random.uniform(part_keys[2], (REQS, CTX), jnp.float32) ** levels(part_keys[2], (REQS, CTX), ((0, 2), (1, 4)), -0.2, 0.2)), 1.5, 12.0),
        "lengths": draw_lengths(jax.random.fold_in(jax.random.fold_in(keys[9], part), 71), part),
        "owners": draw_owners(jax.random.fold_in(jax.random.fold_in(keys[9], part), 71), part),
        "selected": draw_selected(jax.random.fold_in(jax.random.fold_in(keys[9], part), 71), part),
        "query": draw_query(jax.random.fold_in(jax.random.fold_in(keys[9], part), 71), part),
        "index_query": centred(part_keys[7], (STEPS, SLOTS, IH, IDK), IDK ** -0.5, 0.5, ((1, 8),)),
        "index_weight": centred(part_keys[8], (STEPS, SLOTS, IH), IH ** -0.5, 0.75, ((1, 8),)),
    }


score_scale = 192.0 ** -0.5
masked_value = -1.0e30


def reference(cache, index_key, index_scale, lengths, owners, selected, query, index_query, index_weight):
    requests = jnp.arange(REQS, dtype=jnp.int32)
    slot_of = (owners * N_REQ + requests // REQ_COL).astype(jnp.int32)
    positions = jnp.arange(CTX, dtype=jnp.int32)

    def per_request(request):
        slot_index = slot_of[request]
        index_rows = index_key[request]
        request_rows = cache[request]
        length = lengths[request]
        score_list = []
        top_list = []
        output_list = []
        for step_index in range(STEPS):
            heads_query = index_query[step_index, slot_index]
            raw_dots = jnp.dot(heads_query, index_rows.T, preferred_element_type=jnp.float32)
            head_weight = index_weight[step_index, slot_index].astype(jnp.float32)
            weighted = jnp.sum(jax.nn.relu(raw_dots) * head_weight[:, None], axis=0)
            scores = weighted * index_scale[request]
            in_length = positions < length + step_index
            score_list.append(jnp.where(in_length, scores, 0.0))
            ranked = lax.top_k(jnp.where(in_length, scores, masked_value), TOPK)[0]
            top_list.append(ranked[TOPK - 1])
            picked_rows = jnp.take(request_rows, selected[step_index, request], axis=0)
            logits = jnp.dot(query[step_index, slot_index], picked_rows.T, preferred_element_type=jnp.float32) * score_scale
            row_peak = jnp.max(logits, axis=1, keepdims=True)
            weights = jnp.exp(logits - row_peak)
            row_total = jnp.sum(weights, axis=1, keepdims=True)
            mixture = jnp.dot(weights.astype(jnp.bfloat16), picked_rows[:, :LAT], preferred_element_type=jnp.float32)
            output_list.append((mixture / row_total).astype(jnp.bfloat16))
        return jnp.stack(score_list), jnp.stack(top_list), jnp.stack(output_list)

    all_scores, all_tops, outputs = lax.map(per_request, requests)
    attended = jnp.zeros((STEPS, SLOTS, H, LAT), jnp.bfloat16)
    attended = attended.at[:, slot_of].set(jnp.transpose(outputs, (1, 0, 2, 3)))
    return jnp.transpose(all_scores, (1, 0, 2)), jnp.transpose(all_tops, (1, 0)), attended
```

```python
import functools

import jax
import jax.numpy as jnp
from jax import lax
from jax.experimental import pallas as pl
from jax.experimental.pallas import tpu as pltpu
from jax.sharding import PartitionSpec as P

ROPE = 64
LANES = 128
SUBLANES = 8
STAT_ROWS = 16


score_scale = 192.0 ** (-0.5)
masked_value = -1e30
lowest_peak = -1e29
SEARCH_STEPS = 8
SEARCH_WAYS = 8

F32 = jnp.float32
BF16 = jnp.bfloat16


def vmem():
    return pl.BlockSpec(memory_space=pltpu.VMEM)


def smem():
    return pl.BlockSpec(memory_space=pltpu.SMEM)


def dot_nt(a, b):
    return lax.dot_general(a, b, (((1,), (1,)), ((), ())), preferred_element_type=F32)


def query_rows(width, rows):
    full, rest = divmod(width, LANES)
    return full * rows + (rows * rest) // LANES


def pack_kernel(query_ref, index_query_ref, index_weight_ref, out_ref):
    steps, _, heads, width = query_ref.shape
    index_heads = index_query_ref.shape[2]
    rows = steps * heads
    full, rest = divmod(width, LANES)
    for step in range(steps):
        for chunk in range(full):
            out_ref[chunk * rows + step * heads : chunk * rows + (step + 1) * heads, :] = query_ref[
                step, 0, :, chunk * LANES : (chunk + 1) * LANES
            ]
    at = full * rows
    if rest:
        fold = LANES // rest
        tail = jnp.concatenate(
            [query_ref[step, 0, :, full * LANES :] for step in range(steps)], axis=0
        )
        count = rows // fold
        out_ref[at : at + count, :] = jnp.concatenate(
            [tail[part * count : (part + 1) * count] for part in range(fold)], axis=1
        )
        at += count
    for step in range(steps):
        out_ref[at : at + index_heads, :] = index_query_ref[step, 0]
        at += index_heads
    weights = jnp.concatenate([index_weight_ref[step].astype(F32) for step in range(steps)], axis=1)
    out_ref[at : at + STAT_ROWS, :] = jnp.broadcast_to(
        weights, (STAT_ROWS, weights.shape[1])
    ).astype(BF16)


def pack_queries(query, index_query, index_weight):
    steps, _, heads, width = query.shape
    index_rows = steps * index_query.shape[2]
    rows = query_rows(width, steps * heads) + index_rows + STAT_ROWS
    return pl.pallas_call(
        pack_kernel,
        out_shape=jax.ShapeDtypeStruct((rows, LANES), BF16),
        in_specs=[vmem()] * 3,
        out_specs=vmem(),
        name="pack_queries",
    )(query, index_query, index_weight)


def bias_kernel(selected_ref, bias_ref):
    requests, steps, shard_rows = bias_ref.shape
    first = lax.axis_index("seq") * shard_rows
    chunks = shard_rows // LANES
    high_rows = -(-chunks // SUBLANES) * SUBLANES
    count = selected_ref.shape[2]
    for request in range(requests):
        for step in range(steps):
            local = selected_ref[step, request : request + 1, :] - first
            high = local >> 7
            low = local & (LANES - 1)
            high_hot = (lax.broadcasted_iota(jnp.int32, (high_rows, count), 0) == high).astype(F32)
            low_hot = (lax.broadcasted_iota(jnp.int32, (LANES, count), 0) == low).astype(F32)
            hits = dot_nt(high_hot.astype(BF16), low_hot.astype(BF16))
            bias = jnp.where(hits > 0.5, 0.0, masked_value)
            for chunk in range(chunks):
                bias_ref[request, step : step + 1, chunk * LANES : (chunk + 1) * LANES] = bias[
                    chunk : chunk + 1, :
                ]


def selection_bias(selected, shard_rows):
    steps, requests, count = selected.shape
    return pl.pallas_call(
        bias_kernel,
        out_shape=jax.ShapeDtypeStruct((requests, steps, shard_rows), F32),
        in_specs=[vmem()],
        out_specs=vmem(),
        cost_estimate=pl.CostEstimate(
            flops=2 * requests * steps * count * LANES * 16,
            bytes_accessed=requests * steps * (count + shard_rows) * 4,
            transcendentals=0,
        ),
        name="selection_bias",
    )(selected)


def split_three(x):
    high = x.astype(BF16).astype(F32)
    middle = (x - high).astype(BF16).astype(F32)
    return high, middle, x - high - middle


def shard_kernel(seq_count, *refs):
    (owners_ref, lengths_ref), refs = refs[:2], refs[2:]
    sources, refs = refs[:seq_count], refs[seq_count:]
    (key_ref, scale_ref, bias_ref, cache_ref), refs = refs[:4], refs[4:]
    (scores_ref, own_ref, own_stats_ref), refs = refs[:3], refs[3:]
    sends, refs = refs[: seq_count - 1], refs[seq_count - 1 :]
    cache_buf, query_buf, index_buf, candidate_buf, sems = refs

    rank = lax.axis_index("seq")
    requests, width, shard_rows = cache_buf.shape
    steps = scores_ref.shape[0]
    rows = query_buf.shape[1]
    latent = own_ref.shape[1]
    index_rows = index_buf.shape[1] - STAT_ROWS
    index_heads = index_rows // steps
    full, rest = divmod(width, LANES)
    chunks = shard_rows // LANES

    copies = [
        pltpu.make_async_copy(cache_ref.at[request], cache_buf.at[request], sems.at[request])
        for request in range(requests)
    ]
    for copy in copies:
        copy.start()

    for request in range(requests):
        for index, source in enumerate(sources):

            @pl.when(owners_ref[request] == (rank ^ index))
            def _(request=request, source=source):
                for chunk in range(full):
                    query_buf[request, :, chunk * LANES : (chunk + 1) * LANES] = source[
                        chunk * rows : (chunk + 1) * rows, :
                    ]
                at = full * rows
                if rest:
                    fold = LANES // rest
                    count = rows // fold
                    for part in range(fold):
                        query_buf[request, part * count : (part + 1) * count, full * LANES :] = source[
                            at : at + count, part * rest : (part + 1) * rest
                        ]
                    at += count
                index_buf[request] = source[at : at + index_rows + STAT_ROWS, :]

    for request in range(requests):
        dots = dot_nt(index_buf[request, :index_rows, :], key_ref[request])
        weight_row = index_buf[request, index_rows:, :].astype(F32)[:1]
        weight = jnp.transpose(jnp.broadcast_to(weight_row, (LANES, index_rows)))[:, :1]
        terms = jax.nn.relu(dots) * weight
        summed = jnp.concatenate(
            [
                jnp.sum(terms[step * index_heads : (step + 1) * index_heads], axis=0, keepdims=True)
                for step in range(steps)
            ],
            axis=0,
        )
        scores = summed * scale_ref[request : request + 1, :]
        positions = rank * shard_rows + lax.broadcasted_iota(jnp.int32, (steps, shard_rows), 1)
        limit = lengths_ref[request] + lax.broadcasted_iota(jnp.int32, (steps, shard_rows), 0)
        in_length = positions < limit
        scores_ref[:, request, :] = jnp.where(in_length, scores, 0.0)
        candidates = jnp.where(in_length, scores, masked_value)
        for chunk in range(chunks):
            at = (chunk * requests + request) * steps
            candidate_buf[at : at + steps, :] = candidates[:, chunk * LANES : (chunk + 1) * LANES]

    latent_rows = (latent // LANES) * rows
    for request in range(requests):
        copies[request].wait()
        logits = jnp.dot(query_buf[request], cache_buf[request], preferred_element_type=F32)
        bias = jnp.concatenate(
            [
                jnp.broadcast_to(bias_ref[request, step : step + 1, :], (rows // steps, shard_rows))
                for step in range(steps)
            ],
            axis=0,
        )
        logits = logits * score_scale + bias
        peak = jnp.maximum(jnp.max(logits, axis=1, keepdims=True), lowest_peak)
        weights = jnp.exp(logits - peak)
        total = jnp.sum(weights, axis=1, keepdims=True)
        mixture = dot_nt(weights.astype(BF16), cache_buf[request, :latent, :])
        lane = lax.broadcasted_iota(jnp.int32, (rows, LANES), 1)
        stats = jnp.zeros((rows, LANES), F32)
        for index, value in enumerate((*split_three(peak), *split_three(total), peak, total)):
            stats = jnp.where(lane == index, value, stats)
        stats = jnp.transpose(stats)[:STAT_ROWS]

        @pl.when(owners_ref[request] == rank)
        def _(mixture=mixture, stats=stats):
            own_ref[...] = mixture
            own_stats_ref[...] = stats

        packed = mixture.astype(BF16)
        for index, send in enumerate(sends):

            @pl.when(owners_ref[request] == (rank ^ (index + 1)))
            def _(send=send, packed=packed, stats=stats):
                for chunk in range(latent // LANES):
                    send[chunk * rows : (chunk + 1) * rows, :] = packed[
                        :, chunk * LANES : (chunk + 1) * LANES
                    ]
                send[latent_rows : latent_rows + STAT_ROWS, :] = stats.astype(BF16)

    own_candidates = candidate_buf[...].astype(BF16)
    for send in sends:
        send[latent_rows + STAT_ROWS :, :] = own_candidates


def shard_sums(owners, lengths, sources, index_key, index_scale, bias, cache_t, latent):
    seq_count = len(sources)
    requests, width, shard_rows = cache_t.shape
    steps = bias.shape[1]
    rows = LANES
    index_block = sources[0].shape[0] - query_rows(width, rows)
    candidate_rows = requests * steps * (shard_rows // LANES)
    send_rows = (latent // LANES) * rows + STAT_ROWS + candidate_rows
    return pl.pallas_call(
        functools.partial(shard_kernel, seq_count),
        out_shape=(
            jax.ShapeDtypeStruct((steps, requests, shard_rows), F32),
            jax.ShapeDtypeStruct((rows, latent), F32),
            jax.ShapeDtypeStruct((STAT_ROWS, LANES), F32),
        )
        + (jax.ShapeDtypeStruct((send_rows, LANES), BF16),) * (seq_count - 1),
        in_specs=[smem()] * 2 + [vmem()] * (seq_count + 3) + [pl.BlockSpec(memory_space=pl.ANY)],
        out_specs=(vmem(),) * (seq_count + 2),
        scratch_shapes=[
            pltpu.VMEM((requests, width, shard_rows), BF16),
            pltpu.VMEM((requests, rows, width), BF16),
            pltpu.VMEM((requests, index_block, LANES), BF16),
            pltpu.VMEM((candidate_rows, LANES), F32),
            pltpu.SemaphoreType.DMA((requests,)),
        ],
        name="shard_sums",
    )(owners, lengths, *sources, index_key, index_scale, bias, cache_t)


def search_threshold(pieces, lists, keep_count):
    group = max(lists, SUBLANES)
    values = jnp.concatenate(pieces, axis=0)
    values = values.reshape(values.shape[0] // group, group, LANES)

    def across(x, join, lane_join):
        x = lane_join(x, axis=1, keepdims=True)
        shift = lists
        x = jnp.broadcast_to(x, (group, LANES))
        while shift < group:
            x = join(x, pltpu.roll(x, shift, 0))
            shift *= 2
        return x

    low = across(
        jnp.min(jnp.where(values > lowest_peak, values, -masked_value), axis=0), jnp.minimum, jnp.min
    )
    high = across(jnp.max(values, axis=0), jnp.maximum, jnp.max)
    for _ in range(SEARCH_STEPS):
        width = (high - low) * (1.0 / SEARCH_WAYS)
        new_low, new_high = low, high
        for way in range(1, SEARCH_WAYS):
            middle = low + width * way
            count = across(
                jnp.sum((values >= middle[None]).astype(F32), axis=0), jnp.add, jnp.sum
            )
            enough = count >= keep_count
            new_low = jnp.where(enough, jnp.maximum(new_low, middle), new_low)
            new_high = jnp.where(enough, new_high, jnp.minimum(new_high, middle))
        low, high = new_low, new_high
    return across(
        jnp.min(jnp.where(values >= low[None], values, -masked_value), axis=0),
        jnp.minimum,
        jnp.min,
    )


def merge_kernel(seq_count, keep_count, *refs):
    owners_ref, own_ref, own_stats_ref, own_candidates_ref = refs[:4]
    received = refs[4 : 4 + seq_count - 1]
    threshold_ref, attended_ref = refs[4 + seq_count - 1 :]
    rank = lax.axis_index("seq")
    rows, latent = own_ref.shape
    steps, requests = threshold_ref.shape
    latent_rows = (latent // LANES) * rows
    first_candidate = latent_rows + STAT_ROWS

    pieces = [own_candidates_ref[first_candidate:, :].astype(F32)]
    pieces += [ref[first_candidate:, :].astype(F32) for ref in received]
    threshold = search_threshold(pieces, steps * requests, keep_count)
    for request in range(requests):
        for step in range(steps):
            at = request * steps + step
            threshold_ref[step : step + 1, request : request + 1] = threshold[at : at + 1, :1]

    def stat_columns(ref_rows):
        block = jnp.concatenate(
            [ref_rows, jnp.zeros((LANES - ref_rows.shape[0], LANES), F32)], axis=0
        )
        return jnp.transpose(block)

    own_stats = own_stats_ref[...]
    columns = stat_columns(own_stats)
    peaks = [columns[:, 6:7]]
    totals = [columns[:, 7:8]]
    for ref in received:
        columns = stat_columns(ref[latent_rows : latent_rows + STAT_ROWS, :].astype(F32))
        peaks.append(columns[:, 0:1] + columns[:, 1:2] + columns[:, 2:3])
        totals.append(columns[:, 3:4] + columns[:, 4:5] + columns[:, 5:6])
    highest = functools.reduce(jnp.maximum, peaks)
    factors = [jnp.exp(peak - highest) for peak in peaks]
    total = functools.reduce(jnp.add, [a * b for a, b in zip(totals, factors)])
    factors = [factor / total for factor in factors]
    holds = functools.reduce(
        jnp.logical_or, [owners_ref[request] == rank for request in range(requests)]
    )
    heads = rows // steps

    @pl.when(holds)
    def _():
        for chunk in range(latent // LANES):
            part = slice(chunk * LANES, (chunk + 1) * LANES)
            merged = own_ref[:, part] * factors[0]
            for ref, factor in zip(received, factors[1:]):
                merged += ref[chunk * rows : (chunk + 1) * rows, :].astype(F32) * factor
            merged = merged.astype(BF16)
            for step in range(steps):
                attended_ref[step, 0, :, part] = merged[step * heads : (step + 1) * heads]

    @pl.when(jnp.logical_not(holds))
    def _():
        attended_ref[...] = jnp.zeros_like(attended_ref)


def merge(owners, own, own_stats, own_send, received, steps, requests, keep_count):
    seq_count = len(received) + 1
    rows, latent = own.shape
    return pl.pallas_call(
        functools.partial(merge_kernel, seq_count, keep_count),
        out_shape=(
            jax.ShapeDtypeStruct((steps, requests), F32),
            jax.ShapeDtypeStruct((steps, 1, rows // steps, latent), BF16),
        ),
        in_specs=[smem()] + [vmem()] * (seq_count + 2),
        out_specs=(vmem(), vmem()),
        name="merge",
    )(owners, own, own_stats, own_send, *received)


def shards(
    cache, index_key, index_scale, lengths, owners, selected, query, index_query, index_weight
):
    seq_count = lax.axis_size("seq")
    requests, shard_rows, width = cache.shape
    steps, _, keep_count = selected.shape
    latent = width - ROPE
    cache_t = jnp.transpose(cache, (0, 2, 1))

    def exchange(x, bit):
        return lax.ppermute(x, "seq", [(place, place ^ bit) for place in range(seq_count)])

    packed = pack_queries(query, index_query, index_weight)
    sources = [packed] + [exchange(packed, bit) for bit in range(1, seq_count)]
    bias = selection_bias(selected, shard_rows)
    index_scores, own, own_stats, *sends = shard_sums(
        owners, lengths, sources, index_key, index_scale, bias, cache_t, latent
    )
    received = [exchange(send, bit) for bit, send in enumerate(sends, 1)]
    threshold, attended = merge(
        owners, own, own_stats, sends[0], received, steps, requests, keep_count
    )
    return (index_scores, threshold, attended)


def solution(mesh):
    placed = (
        P(("groups", "req"), "seq", None),
        P(("groups", "req"), "seq", None),
        P(("groups", "req"), "seq"),
        P(("groups", "req")),
        P(("groups", "req")),
        P(None, ("groups", "req"), None),
        P(None, ("groups", "seq", "req"), "head", None),
        P(None, ("groups", "seq", "req"), None, None),
        P(None, ("groups", "seq", "req"), None),
    )
    return jax.shard_map(
        shards,
        mesh=mesh,
        in_specs=placed,
        out_specs=(
            P(None, ("groups", "req"), "seq"),
            P(None, ("groups", "req")),
            P(None, ("groups", "seq", "req"), "head", None),
        ),
        check_vma=False,
    )
```

```python
import functools

import jax
import jax.numpy as jnp
from jax import lax
from jax.experimental import pallas as pl
from jax.experimental.pallas import tpu as pltpu
from jax.sharding import PartitionSpec as P

ROPE = 64
LANES = 128
SUBLANES = 8
STAT_ROWS = 16
VMEM_GRANT = 12 * 2**20


score_scale = 192.0 ** (-0.5)
masked_value = -1e30
lowest_peak = -1e29
SEARCH_STEPS = 8
SEARCH_WAYS = 8

F32 = jnp.float32
BF16 = jnp.bfloat16


def vmem():
    return pl.BlockSpec(memory_space=pltpu.VMEM)


def smem():
    return pl.BlockSpec(memory_space=pltpu.SMEM)


def grant():
    return pltpu.CompilerParams(vmem_limit_bytes=VMEM_GRANT)


def dot_nt(a, b):
    return lax.dot_general(a, b, (((1,), (1,)), ((), ())), preferred_element_type=F32)


def query_rows(width, rows):
    full, rest = divmod(width, LANES)
    return full * rows + (rows * rest) // LANES


def pack_kernel(query_ref, index_query_ref, index_weight_ref, out_ref):
    steps, _, heads, width = query_ref.shape
    index_heads = index_query_ref.shape[2]
    rows = steps * heads
    full, rest = divmod(width, LANES)
    for step in range(steps):
        for chunk in range(full):
            out_ref[chunk * rows + step * heads : chunk * rows + (step + 1) * heads, :] = query_ref[
                step, 0, :, chunk * LANES : (chunk + 1) * LANES
            ]
    at = full * rows
    if rest:
        fold = LANES // rest
        tail = jnp.concatenate(
            [query_ref[step, 0, :, full * LANES :] for step in range(steps)], axis=0
        )
        count = rows // fold
        out_ref[at : at + count, :] = jnp.concatenate(
            [tail[part * count : (part + 1) * count] for part in range(fold)], axis=1
        )
        at += count
    for step in range(steps):
        out_ref[at : at + index_heads, :] = index_query_ref[step, 0]
        at += index_heads
    weights = jnp.concatenate([index_weight_ref[:, step].astype(F32) for step in range(steps)], axis=1)
    out_ref[at : at + STAT_ROWS, :] = jnp.broadcast_to(
        weights, (STAT_ROWS, weights.shape[1])
    ).astype(BF16)


def pack_queries(query, index_query, index_weight):
    steps, _, heads, width = query.shape
    index_rows = steps * index_query.shape[2]
    rows = query_rows(width, steps * heads) + index_rows + STAT_ROWS
    return pl.pallas_call(
        pack_kernel,
        out_shape=jax.ShapeDtypeStruct((rows, LANES), BF16),
        in_specs=[vmem()] * 3,
        out_specs=vmem(),
        compiler_params=grant(),
        name="pack_queries",
    )(query, index_query, index_weight)


def bias_kernel(selected_ref, cache_ref, bias_ref, staged_ref, sem):
    copy = pltpu.make_async_copy(cache_ref, staged_ref, sem)
    copy.start()
    requests, steps, shard_rows = bias_ref.shape
    first = lax.axis_index("seq") * shard_rows
    chunks = shard_rows // LANES
    high_rows = -(-chunks // SUBLANES) * SUBLANES
    count = selected_ref.shape[2]
    for request in range(requests):
        for step in range(steps):
            local = selected_ref[step, request : request + 1, :] - first
            high = local >> 7
            low = local & (LANES - 1)
            high_hot = (lax.broadcasted_iota(jnp.int32, (high_rows, count), 0) == high).astype(F32)
            low_hot = (lax.broadcasted_iota(jnp.int32, (LANES, count), 0) == low).astype(F32)
            hits = dot_nt(high_hot.astype(BF16), low_hot.astype(BF16))
            bias = jnp.where(hits > 0.5, 0.0, masked_value)
            for chunk in range(chunks):
                bias_ref[request, step : step + 1, chunk * LANES : (chunk + 1) * LANES] = bias[
                    chunk : chunk + 1, :
                ]
    copy.wait()


def selection_bias(selected, cache_t):
    steps, requests, count = selected.shape
    shard_rows = cache_t.shape[2]
    return pl.pallas_call(
        bias_kernel,
        out_shape=(
            jax.ShapeDtypeStruct((requests, steps, shard_rows), F32),
            jax.ShapeDtypeStruct(cache_t.shape, cache_t.dtype),
        ),
        in_specs=[vmem(), pl.BlockSpec(memory_space=pl.ANY)],
        out_specs=(vmem(), vmem()),
        scratch_shapes=[pltpu.SemaphoreType.DMA],
        cost_estimate=pl.CostEstimate(
            flops=2 * requests * steps * count * LANES * 16,
            bytes_accessed=requests * steps * (count + shard_rows) * 4,
            transcendentals=0,
        ),
        compiler_params=grant(),
        name="selection_bias",
    )(selected, cache_t)


def split_three(x):
    high = x.astype(BF16).astype(F32)
    middle = (x - high).astype(BF16).astype(F32)
    return high, middle, x - high - middle


def shard_kernel(seq_count, *refs):
    (owners_ref, lengths_ref), refs = refs[:2], refs[2:]
    sources, refs = refs[:seq_count], refs[seq_count:]
    (key_ref, scale_ref, bias_ref, cache_ref), refs = refs[:4], refs[4:]
    (scores_ref, own_ref, own_stats_ref), refs = refs[:3], refs[3:]
    sends, refs = refs[: seq_count - 1], refs[seq_count - 1 :]
    query_buf, index_buf, candidate_buf = refs

    rank = lax.axis_index("seq")
    requests, width, shard_rows = cache_ref.shape
    steps = scores_ref.shape[0]
    rows = query_buf.shape[1]
    latent = own_ref.shape[1]
    index_rows = index_buf.shape[1] - STAT_ROWS
    index_heads = index_rows // steps
    full, rest = divmod(width, LANES)
    chunks = shard_rows // LANES

    for request in range(requests):
        for index, source in enumerate(sources):

            @pl.when(owners_ref[request] == (rank ^ index))
            def _(request=request, source=source):
                for chunk in range(full):
                    query_buf[request, :, chunk * LANES : (chunk + 1) * LANES] = source[
                        chunk * rows : (chunk + 1) * rows, :
                    ]
                at = full * rows
                if rest:
                    fold = LANES // rest
                    count = rows // fold
                    for part in range(fold):
                        query_buf[request, part * count : (part + 1) * count, full * LANES :] = source[
                            at : at + count, part * rest : (part + 1) * rest
                        ]
                    at += count
                index_buf[request] = source[at : at + index_rows + STAT_ROWS, :]

    for request in range(requests):
        dots = dot_nt(index_buf[request, :index_rows, :], key_ref[request])
        weight_row = index_buf[request, index_rows:, :].astype(F32)[:1]
        weight = jnp.transpose(jnp.broadcast_to(weight_row, (LANES, index_rows)))[:, :1]
        terms = jax.nn.relu(dots) * weight
        summed = jnp.concatenate(
            [
                jnp.sum(terms[step * index_heads : (step + 1) * index_heads], axis=0, keepdims=True)
                for step in range(steps)
            ],
            axis=0,
        )
        scores = summed * scale_ref[request : request + 1, :]
        positions = rank * shard_rows + lax.broadcasted_iota(jnp.int32, (steps, shard_rows), 1)
        limit = lengths_ref[request] + lax.broadcasted_iota(jnp.int32, (steps, shard_rows), 0)
        in_length = positions < limit
        scores_ref[:, request, :] = jnp.where(in_length, scores, 0.0)
        candidates = jnp.where(in_length, scores, masked_value)
        for chunk in range(chunks):
            at = (chunk * requests + request) * steps
            candidate_buf[at : at + steps, :] = candidates[:, chunk * LANES : (chunk + 1) * LANES]

    latent_rows = (latent // LANES) * rows
    for request in range(requests):
        logits = jnp.dot(query_buf[request], cache_ref[request], preferred_element_type=F32)
        bias = jnp.concatenate(
            [
                jnp.broadcast_to(bias_ref[request, step : step + 1, :], (rows // steps, shard_rows))
                for step in range(steps)
            ],
            axis=0,
        )
        logits = logits * score_scale + bias
        peak = jnp.maximum(jnp.max(logits, axis=1, keepdims=True), lowest_peak)
        weights = jnp.exp(logits - peak)
        total = jnp.sum(weights, axis=1, keepdims=True)
        mixture = dot_nt(weights.astype(BF16), cache_ref[request, :latent, :])
        lane = lax.broadcasted_iota(jnp.int32, (rows, LANES), 1)
        stats = jnp.zeros((rows, LANES), F32)
        for index, value in enumerate((*split_three(peak), *split_three(total), peak, total)):
            stats = jnp.where(lane == index, value, stats)
        stats = jnp.transpose(stats)[:STAT_ROWS]

        @pl.when(owners_ref[request] == rank)
        def _(mixture=mixture, stats=stats):
            own_ref[...] = mixture
            own_stats_ref[...] = stats

        packed = mixture.astype(BF16)
        for index, send in enumerate(sends):

            @pl.when(owners_ref[request] == (rank ^ (index + 1)))
            def _(send=send, packed=packed, stats=stats):
                for chunk in range(latent // LANES):
                    send[chunk * rows : (chunk + 1) * rows, :] = packed[
                        :, chunk * LANES : (chunk + 1) * LANES
                    ]
                send[latent_rows : latent_rows + STAT_ROWS, :] = stats.astype(BF16)

    own_candidates = candidate_buf[...].astype(BF16)
    for send in sends:
        send[latent_rows + STAT_ROWS :, :] = own_candidates


def shard_sums(owners, lengths, sources, index_key, index_scale, bias, cache_t, latent):
    seq_count = len(sources)
    requests, width, shard_rows = cache_t.shape
    steps = bias.shape[1]
    rows = LANES
    index_block = sources[0].shape[0] - query_rows(width, rows)
    candidate_rows = requests * steps * (shard_rows // LANES)
    send_rows = (latent // LANES) * rows + STAT_ROWS + candidate_rows
    return pl.pallas_call(
        functools.partial(shard_kernel, seq_count),
        out_shape=(
            jax.ShapeDtypeStruct((steps, requests, shard_rows), F32),
            jax.ShapeDtypeStruct((rows, latent), F32),
            jax.ShapeDtypeStruct((STAT_ROWS, LANES), F32),
        )
        + (jax.ShapeDtypeStruct((send_rows, LANES), BF16),) * (seq_count - 1),
        in_specs=[smem()] * 2 + [vmem()] * (seq_count + 4),
        out_specs=(vmem(),) * (seq_count + 2),
        scratch_shapes=[
            pltpu.VMEM((requests, rows, width), BF16),
            pltpu.VMEM((requests, index_block, LANES), BF16),
            pltpu.VMEM((candidate_rows, LANES), F32),
        ],
        compiler_params=grant(),
        name="shard_sums",
    )(owners, lengths, *sources, index_key, index_scale, bias, cache_t)


def search_threshold(pieces, lists, keep_count):
    group = max(lists, SUBLANES)
    values = jnp.concatenate(pieces, axis=0)
    values = values.reshape(values.shape[0] // group, group, LANES)

    def across(x, join, lane_join):
        x = lane_join(x, axis=1, keepdims=True)
        shift = lists
        x = jnp.broadcast_to(x, (group, LANES))
        while shift < group:
            x = join(x, pltpu.roll(x, shift, 0))
            shift *= 2
        return x

    low = across(
        jnp.min(jnp.where(values > lowest_peak, values, -masked_value), axis=0), jnp.minimum, jnp.min
    )
    high = across(jnp.max(values, axis=0), jnp.maximum, jnp.max)
    for _ in range(SEARCH_STEPS):
        width = (high - low) * (1.0 / SEARCH_WAYS)
        new_low, new_high = low, high
        for way in range(1, SEARCH_WAYS):
            middle = low + width * way
            count = across(
                jnp.sum((values >= middle[None]).astype(F32), axis=0), jnp.add, jnp.sum
            )
            enough = count >= keep_count
            new_low = jnp.where(enough, jnp.maximum(new_low, middle), new_low)
            new_high = jnp.where(enough, new_high, jnp.minimum(new_high, middle))
        low, high = new_low, new_high
    return across(
        jnp.min(jnp.where(values >= low[None], values, -masked_value), axis=0),
        jnp.minimum,
        jnp.min,
    )


def merge_kernel(seq_count, keep_count, *refs):
    owners_ref, own_ref, own_stats_ref, own_candidates_ref = refs[:4]
    received = refs[4 : 4 + seq_count - 1]
    threshold_ref, attended_ref = refs[4 + seq_count - 1 :]
    rank = lax.axis_index("seq")
    rows, latent = own_ref.shape
    steps, requests = threshold_ref.shape
    latent_rows = (latent // LANES) * rows
    first_candidate = latent_rows + STAT_ROWS

    pieces = [own_candidates_ref[first_candidate:, :].astype(F32)]
    pieces += [ref[first_candidate:, :].astype(F32) for ref in received]
    threshold = search_threshold(pieces, steps * requests, keep_count)
    for request in range(requests):
        for step in range(steps):
            at = request * steps + step
            threshold_ref[step : step + 1, request : request + 1] = threshold[at : at + 1, :1]

    def stat_columns(ref_rows):
        block = jnp.concatenate(
            [ref_rows, jnp.zeros((LANES - ref_rows.shape[0], LANES), F32)], axis=0
        )
        return jnp.transpose(block)

    own_stats = own_stats_ref[...]
    columns = stat_columns(own_stats)
    peaks = [columns[:, 6:7]]
    totals = [columns[:, 7:8]]
    for ref in received:
        columns = stat_columns(ref[latent_rows : latent_rows + STAT_ROWS, :].astype(F32))
        peaks.append(columns[:, 0:1] + columns[:, 1:2] + columns[:, 2:3])
        totals.append(columns[:, 3:4] + columns[:, 4:5] + columns[:, 5:6])
    highest = functools.reduce(jnp.maximum, peaks)
    factors = [jnp.exp(peak - highest) for peak in peaks]
    total = functools.reduce(jnp.add, [a * b for a, b in zip(totals, factors)])
    factors = [factor / total for factor in factors]
    holds = functools.reduce(
        jnp.logical_or, [owners_ref[request] == rank for request in range(requests)]
    )
    heads = rows // steps

    @pl.when(holds)
    def _():
        for chunk in range(latent // LANES):
            part = slice(chunk * LANES, (chunk + 1) * LANES)
            merged = own_ref[:, part] * factors[0]
            for ref, factor in zip(received, factors[1:]):
                merged += ref[chunk * rows : (chunk + 1) * rows, :].astype(F32) * factor
            merged = merged.astype(BF16)
            for step in range(steps):
                attended_ref[step, 0, :, part] = merged[step * heads : (step + 1) * heads]

    @pl.when(jnp.logical_not(holds))
    def _():
        attended_ref[...] = jnp.zeros_like(attended_ref)


def merge(owners, own, own_stats, own_send, received, steps, requests, keep_count):
    seq_count = len(received) + 1
    rows, latent = own.shape
    return pl.pallas_call(
        functools.partial(merge_kernel, seq_count, keep_count),
        out_shape=(
            jax.ShapeDtypeStruct((steps, requests), F32),
            jax.ShapeDtypeStruct((steps, 1, rows // steps, latent), BF16),
        ),
        in_specs=[smem()] + [vmem()] * (seq_count + 2),
        out_specs=(vmem(), vmem()),
        compiler_params=grant(),
        name="merge",
    )(owners, own, own_stats, own_send, *received)


def shards(
    cache, index_key, index_scale, lengths, owners, selected, query, index_query, index_weight
):
    seq_count = lax.axis_size("seq")
    requests, shard_rows, width = cache.shape
    steps, _, keep_count = selected.shape
    latent = width - ROPE
    cache_t = jnp.transpose(cache, (0, 2, 1))

    def exchange(x, bit):
        return lax.ppermute(x, "seq", [(place, place ^ bit) for place in range(seq_count)])

    packed = pack_queries(query, index_query, jnp.transpose(index_weight, (1, 0, 2)))
    sources = [packed] + [exchange(packed, bit) for bit in range(1, seq_count)]
    bias, staged = selection_bias(selected, cache_t)
    index_scores, own, own_stats, *sends = shard_sums(
        owners, lengths, sources, index_key, index_scale, bias, staged, latent
    )
    received = [exchange(send, bit) for bit, send in enumerate(sends, 1)]
    threshold, attended = merge(
        owners, own, own_stats, sends[0], received, steps, requests, keep_count
    )
    return (index_scores, threshold, attended)


def solution(mesh):
    placed = (
        P(("groups", "req"), "seq", None),
        P(("groups", "req"), "seq", None),
        P(("groups", "req"), "seq"),
        P(("groups", "req")),
        P(("groups", "req")),
        P(None, ("groups", "req"), None),
        P(None, ("groups", "seq", "req"), "head", None),
        P(None, ("groups", "seq", "req"), None, None),
        P(None, ("groups", "seq", "req"), None),
    )
    return jax.shard_map(
        shards,
        mesh=mesh,
        in_specs=placed,
        out_specs=(
            P(None, ("groups", "req"), "seq"),
            P(None, ("groups", "req")),
            P(None, ("groups", "seq", "req"), "head", None),
        ),
        check_vma=False,
    )
```
